32 devices in a mesh: real: 4 (over z), rows: 4 (over y, core), field: 2 (over x).
Axes of the slice: x: 2, y: 2, z: 4, core: 2. Of those that a mesh axis runs over, the one named last changes fastest.
Arguments:
- sims: bfloat16 [4, 2, 2048, 2048], P('real', 'field', 'rows'), may hold values from -6 to 6
- data: bfloat16 [2, 2048, 2048], P('field', 'rows'), may hold values from -6 to 6
- mask_flags: int32 [16, 16], P('rows'), may hold values 0 or 1
- bins: int32 [512, 512], P(None, 'rows'), may hold values from 0 to 63
- cl_signal: float32 [2, 64], P('field'), may hold values from 0.5 to 4
- cl_noise: float32 [2, 64], P('field'), may hold values from 0.1 to 2
- norm: float32 [64], replicated, may hold values from 0.5 to 2
- matching: int32 [4], replicated, may hold values from 0 to 3, each once
Outputs:
- estimates: float32 [4, 2, 2, 512, 512], P('real', None, None, None, 'rows')
The draws below stay inside these ranges and needn't reach their ends.
Inputs may be any that keep to these rules, and one draw needn't show every extreme that they name: `matching`: each realization index appears exactly once.
All inputs are finite; a program needn't handle non-finite values. No bound on the sum of `mask_flags` on one device may be relied on, other than what follows from the above.
Results may differ from the reference program's by a relative error of at most 0.011.
Values may be sent and summed in bfloat16 or wider, within the bound.
A program may use at most 128 MiB of HBM per device.

```python
import math
import jax
import jax.numpy as jnp
from jax import lax

NPIX = 2048
KF = 512
NB = 64
TILE = 128
FIELDS = 2
REALS = 4


def with_ends(entries, stream_key, least, high):
    longest = entries.shape.index(max(entries.shape))
    spots = []
    for shift in (0, 1):
        where = [jax.random.randint(jax.random.fold_in(stream_key, axis), (), 0, length) for axis, length in enumerate(entries.shape)]
        where[longest] = (where[longest] + shift) % entries.shape[longest]
        spots.append(tuple(where))
    return entries.at[spots[0]].set(least).at[spots[1]].set(high)


def block_scale(key, extent, cuts, least, high):
    level, own = 1.0, jax.random.fold_in(key, 6)
    for dim, shards_of in cuts:
        draws = jnp.exp(jax.random.uniform(jax.random.fold_in(own, dim), (shards_of,), jnp.float32, least / len(cuts), high / len(cuts)))
        level = level * jnp.repeat(draws, extent[dim] // shards_of).reshape([-1 if axis == dim else 1 for axis in range(len(extent))])
    return level


def noise(stream_key, extent, scale, bound, pieces=(), kind=jnp.bfloat16):
    factor_of = block_scale(stream_key, extent, pieces, -0.22, 0.18) if pieces else 1.0
    values = jax.random.normal(stream_key, extent, jnp.float32) * scale * factor_of
    return jnp.minimum(jnp.maximum(values, -bound), bound).astype(kind)


def setup_inputs(seed: int = 0) -> dict:
    arg_keys = jax.random.split(jax.random.key(seed), 9)
    sims = noise(arg_keys[0], (REALS, FIELDS, NPIX, NPIX), 1.0, 6.0, ((0, 4), (1, 2), (2, 4)))
    data = noise(arg_keys[1], (FIELDS, NPIX, NPIX), 1.0, 6.0, ((0, 2), (1, 4)))
    mask_flags = with_ends((jax.random.randint(arg_keys[2], (NPIX // TILE, NPIX // TILE), 0, 8) < 7).astype(jnp.int32), jax.random.fold_in(arg_keys[2], 1), 0, 1)
    bins = with_ends(jax.random.randint(arg_keys[3], (KF, KF), 0, NB), jax.random.fold_in(arg_keys[3], 1), 0, NB - 1).astype(jnp.int32)
    cl_signal = jnp.clip(jnp.exp(math.log(4.0) - 2.0794415 * jax.random.uniform(arg_keys[4], (FIELDS, NB), jnp.float32) ** block_scale(arg_keys[4], (FIELDS, NB), ((0, 2),), -0.2, 0.2)), 0.5, 4.0)
    cl_noise = jnp.clip(jnp.exp(math.log(2.0) - 2.9957323 * jax.random.uniform(arg_keys[5], (FIELDS, NB), jnp.float32) ** block_scale(arg_keys[5], (FIELDS, NB), ((0, 2),), -0.2, 0.2)), 0.1, 2.0)
    norm = jnp.clip(jnp.exp(jax.random.uniform(arg_keys[6], (NB,), jnp.float32, math.log(0.5), math.log(2.0))), 0.5, 2.0)
    matching = jax.random.permutation(arg_keys[7], REALS).astype(jnp.int32)
    return {"sims": sims, "data": data, "mask_flags": mask_flags, "bins": bins, "cl_signal": cl_signal, "cl_noise": cl_noise, "norm": norm, "matching": matching}


HIGH = lax.Precision.HIGHEST


def tables(npix, kf, scale):
    pixel = jnp.arange(npix, dtype=jnp.int32)
    freq = jnp.arange(kf, dtype=jnp.int32) - kf // 2
    phase = jnp.mod(pixel[:, None] * freq[None, :], npix)
    angle = phase.astype(jnp.float32) * (2.0 * math.pi / npix)
    return (jnp.cos(angle) * scale).astype(jnp.bfloat16), (jnp.sin(angle) * scale).astype(jnp.bfloat16)


def expand_mask(flags, tile):
    first, second = flags.shape
    full = jnp.broadcast_to(flags[:, None, :, None], (first, tile, second, tile))
    return full.reshape(first * tile, second * tile) > 0


def column_part(maps, cos_t, sin_t):
    count, height, width = maps.shape
    flat = maps.reshape(count * height, width)
    a_re = jnp.dot(flat, cos_t, preferred_element_type=jnp.float32).astype(jnp.bfloat16).reshape(count, height, -1)
    a_im = (-jnp.dot(flat, sin_t, preferred_element_type=jnp.float32)).astype(jnp.bfloat16).reshape(count, height, -1)
    return a_re, a_im


def row_part(a_re, a_im, cos_t, sin_t):
    cos_w = cos_t.astype(jnp.float32)
    sin_w = sin_t.astype(jnp.float32)
    are = a_re.astype(jnp.float32)
    aim = a_im.astype(jnp.float32)
    x_re = jnp.einsum('yk,myj->mkj', cos_w, are, precision=HIGH) + jnp.einsum('yk,myj->mkj', sin_w, aim, precision=HIGH)
    x_im = jnp.einsum('yk,myj->mkj', cos_w, aim, precision=HIGH) - jnp.einsum('yk,myj->mkj', sin_w, are, precision=HIGH)
    return x_re, x_im


def forward(maps, cos_t, sin_t):
    a_re, a_im = column_part(maps, cos_t, sin_t)
    return row_part(a_re, a_im, cos_t, sin_t)


def inverse(z_re, z_im, icos, isin):
    count = z_re.shape[0]
    icw = icos.astype(jnp.float32)
    isw = isin.astype(jnp.float32)
    zr = z_re.astype(jnp.float32)
    zi = z_im.astype(jnp.float32)
    y_re = (jnp.einsum('yk,mkj->myj', icw, zr, precision=HIGH) - jnp.einsum('yk,mkj->myj', isw, zi, precision=HIGH)).astype(jnp.bfloat16)
    y_im = (jnp.einsum('yk,mkj->myj', icw, zi, precision=HIGH) + jnp.einsum('yk,mkj->myj', isw, zr, precision=HIGH)).astype(jnp.bfloat16)
    height = y_re.shape[1]
    flat_re = y_re.reshape(count * height, -1)
    flat_im = y_im.reshape(count * height, -1)
    out = jnp.dot(flat_re, icos.T, preferred_element_type=jnp.float32) - jnp.dot(flat_im, isin.T, preferred_element_type=jnp.float32)
    return out.astype(jnp.bfloat16).reshape(count, height, -1)


def filter_legs(x_re, x_im, wcell, gcell, lx, ly):
    grad_x = lx * gcell
    grad_y = ly * gcell
    z_re = jnp.stack([wcell * x_re, -grad_x * x_im, -grad_y * x_im])
    z_im = jnp.stack([wcell * x_im, grad_x * x_re, grad_y * x_re])
    return z_re.astype(jnp.bfloat16), z_im.astype(jnp.bfloat16)


def reference(sims, data, mask_flags, bins, cl_signal, cl_noise, norm, matching):
    mask = expand_mask(mask_flags, TILE)
    cos_t, sin_t = tables(NPIX, KF, NPIX ** -0.5)
    icos, isin = tables(NPIX, KF, KF ** -0.5)
    freq = (jnp.arange(KF, dtype=jnp.int32) - KF // 2).astype(jnp.float32) * (2.0 * math.pi / NPIX)
    lx = jnp.broadcast_to(freq[None, :], (KF, KF))
    ly = jnp.broadcast_to(freq[:, None], (KF, KF))
    weight_vals = 1.0 / (cl_signal + cl_noise)
    grad_vals = cl_signal * weight_vals
    wcell = weight_vals[:, bins]
    gcell = grad_vals[:, bins]
    ncell = norm[bins]

    def legs_of(maps):
        masked = jnp.where(mask[None], maps, jnp.zeros_like(maps))
        x_re, x_im = forward(masked, cos_t, sin_t)
        parts = [filter_legs(x_re[f], x_im[f], wcell[f], gcell[f], lx, ly) for f in range(FIELDS)]
        z_re = jnp.concatenate([p[0] for p in parts], axis=0)
        z_im = jnp.concatenate([p[1] for p in parts], axis=0)
        return inverse(z_re, z_im, icos, isin).reshape(FIELDS, 3, NPIX, NPIX)

    sim_legs = lax.map(legs_of, sims)
    data_legs = legs_of(data).astype(jnp.float32)

    def estimate(index):
        own = sim_legs[index].astype(jnp.float32)
        other = sim_legs[matching[index]].astype(jnp.float32)
        ds_x = data_legs[:, 1] * own[:, 0] + own[:, 1] * data_legs[:, 0]
        ss_x = own[:, 1] * other[:, 0] + other[:, 1] * own[:, 0]
        ds_y = data_legs[:, 2] * own[:, 0] + own[:, 2] * data_legs[:, 0]
        ss_y = own[:, 2] * other[:, 0] + other[:, 2] * own[:, 0]
        products = jnp.stack([ds_x, ss_x, ds_y, ss_y], axis=1).astype(jnp.bfloat16)
        sum_re = jnp.zeros((4, NPIX, KF), jnp.float32)
        sum_im = jnp.zeros((4, NPIX, KF), jnp.float32)
        for f in range(FIELDS):
            part_re, part_im = column_part(products[f], cos_t, sin_t)
            sum_re = sum_re + part_re.astype(jnp.float32)
            sum_im = sum_im + part_im.astype(jnp.float32)
        s_re, s_im = row_part(sum_re.astype(jnp.bfloat16), sum_im.astype(jnp.bfloat16), cos_t, sin_t)
        scale_x = ncell * lx
        scale_y = ncell * ly
        out_re = -scale_x * s_im[0:2] + -scale_y * s_im[2:4]
        out_im = scale_x * s_re[0:2] + scale_y * s_re[2:4]
        return jnp.stack([out_re, out_im], axis=1)

    return lax.map(estimate, jnp.arange(REALS, dtype=jnp.int32))
```

```python
import functools
import math

import jax
import jax.numpy as jnp
import numpy as np
from jax import lax
from jax.experimental import pallas as pl
from jax.experimental.pallas import tpu as pltpu
from jax.sharding import PartitionSpec as P

TILE = 128
BF = jnp.bfloat16
F32 = jnp.float32
VMEM_LIMIT = 60 * 1024 * 1024


def cis(pixels, freqs, npix):
    phase = jnp.mod(pixels[:, None] * freqs[None, :], npix)
    angle = phase.astype(F32) * (2.0 * math.pi / npix)
    return jnp.cos(angle), jnp.sin(angle)


def outer_cis(start, count, freqs, npix):
    low = 32
    freqs = jnp.asarray(freqs, jnp.int32)
    c1, s1 = cis(start + low * jnp.arange(count // low, dtype=jnp.int32), freqs, npix)
    c0, s0 = cis(jnp.arange(low, dtype=jnp.int32), freqs, npix)
    c1, s1, c0, s0 = lax.optimization_barrier((c1, s1, c0, s0))
    c1, s1, c0, s0 = c1[:, None], s1[:, None], c0[None], s0[None]
    width = freqs.shape[0]
    return (
        (c1 * c0 - s1 * s0).reshape(count, width),
        (s1 * c0 + c1 * s0).reshape(count, width),
    )


def lookup_kernel(idx_ref, tab_ref, *outs):
    idx = idx_ref[...].astype(jnp.int32)
    for t, out in enumerate(outs):
        table = jnp.broadcast_to(tab_ref[t : t + 1, :], idx.shape)
        out[...] = jnp.take_along_axis(table, idx, axis=1, mode="promise_in_bounds")


def lookup(idx, values):
    rows, width = idx.shape
    nbins = values[0].shape[0]
    tab = jnp.stack([jnp.pad(v, (0, 128 - nbins)) for v in values])
    tab = jnp.pad(tab, ((0, 8 - len(values)), (0, 0)))
    return pl.pallas_call(
        lookup_kernel,
        out_shape=[jax.ShapeDtypeStruct(idx.shape, F32) for _ in values],
        grid=(width // 128,),
        in_specs=[
            pl.BlockSpec((rows, 128), lambda i: (0, i)),
            pl.BlockSpec((8, 128), lambda i: (0, 0)),
        ],
        out_specs=[pl.BlockSpec((rows, 128), lambda i: (0, i)) for _ in values],
    )(idx, tab)


def ky_kernel(cols, x_ref, w_ref, gx_ref, gy_ref, t_ref, y_ref):
    half = x_ref.shape[2] // 2
    top = y_ref.shape[2] // 2
    x = x_ref[0, 0].astype(F32)
    wide = x.shape[1]
    lane = lax.broadcasted_iota(jnp.int32, x.shape, 1)
    first = (lane & (cols - 1)) < cols // 2
    ix = jnp.where(
        first, -pltpu.roll(x, wide - cols // 2, axis=1), pltpu.roll(x, cols // 2, axis=1)
    )
    w, gx, gy = w_ref[0], gx_ref[0], gy_ref[0]
    pairs = ((w * x, w * ix), (gx * ix, -(gx * x)), (gy * ix, -(gy * x)))
    for leg, (z, iz) in enumerate(pairs):
        z = z.astype(BF)
        iz = iz.astype(BF)
        even = jnp.dot(
            t_ref[0], jnp.concatenate([z[:half], iz[:half]], axis=0), preferred_element_type=F32
        )
        odd = jnp.dot(
            t_ref[1], jnp.concatenate([z[half:], iz[half:]], axis=0), preferred_element_type=F32
        )
        y_ref[0, leg, :top, :] = (even + odd).astype(BF)
        y_ref[0, leg, top:, :] = (even - odd).astype(BF)


def ky_inverse(x, w, gx, gy, table, cols):
    maps, _, kf, wide = x.shape
    top = table.shape[1]
    lanes = 256
    blocks = wide // lanes
    cell = pl.BlockSpec((1, kf, lanes), lambda p, i, m: (p, 0, i))
    return pl.pallas_call(
        functools.partial(ky_kernel, cols),
        out_shape=jax.ShapeDtypeStruct((maps, 3, 2 * top, 2 * wide), BF),
        grid=(2, blocks, maps),
        in_specs=[
            pl.BlockSpec((1, 1, kf, lanes), lambda p, i, m: (m, p, 0, i)),
            cell,
            cell,
            cell,
            pl.BlockSpec(table.shape, lambda p, i, m: (0, 0, 0)),
        ],
        out_specs=pl.BlockSpec(
            (1, 3, 2 * top, lanes), lambda p, i, m: (m, 0, 0, p * blocks + i)
        ),
        compiler_params=pltpu.CompilerParams(vmem_limit_bytes=VMEM_LIMIT),
    )(x, w, gx, gy, table)


def pixel_kernel(xt, y_ref, yp_ref, f_ref, a_ref, legs, prods):
    step = pl.program_id(0)
    height = y_ref.shape[2]
    wide = f_ref.shape[2]
    here = pl.ds(pl.multiple_of(step * xt, xt), xt)
    dims = (((1,), (1,)), ((), ()))

    def make(source, m, leg, slot):
        even = lax.dot_general(
            source[m, leg, :, :wide], f_ref[0, here, :], dims, preferred_element_type=F32
        )
        odd = lax.dot_general(
            source[m, leg, :, wide:], f_ref[1, here, :], dims, preferred_element_type=F32
        )
        legs[0, slot] = (even + odd).astype(BF)
        legs[1, slot] = (even - odd).astype(BF)

    @pl.loop(0, 3)
    def _(leg):
        make(y_ref, 0, leg, leg)
        make(y_ref, 1, leg, leg + 3)
        make(yp_ref, 0, leg, leg + 6)

    chunk = 64

    @pl.loop(0, height // chunk)
    def _(c):
        rows = pl.ds(pl.multiple_of(c * chunk, chunk), chunk)
        sides = []
        for side in range(2):
            own = [legs[side, i, rows, :].astype(F32) for i in range(3)]
            dat = [legs[side, i + 3, rows, :].astype(F32) for i in range(3)]
            par = [legs[side, i + 6, rows, :].astype(F32) for i in range(3)]
            sides.append(
                (
                    dat[1] * own[0] + own[1] * dat[0],
                    own[1] * par[0] + par[1] * own[0],
                    dat[2] * own[0] + own[2] * dat[0],
                    own[2] * par[0] + par[2] * own[0],
                )
            )
        for i in range(4):
            prods[0, i, rows, here] = (sides[0][i] + sides[1][i]).astype(BF)
            prods[1, i, rows, here] = (sides[0][i] - sides[1][i]).astype(BF)

    @pl.when(step == pl.num_programs(0) - 1)
    def _():
        @pl.loop(0, 4)
        def _(i):
            for p in range(2):
                where = pl.ds(pl.multiple_of(i * (2 * wide) + p * wide, wide), wide)
                a_ref[:, where] = jnp.dot(
                    prods[p, i], f_ref[p], preferred_element_type=F32
                ).astype(BF)


def pixel_products(y, yp, table):
    height = y.shape[2]
    pixels, wide = table.shape[1:]
    xt = 256
    whole = lambda a: pl.BlockSpec(
        a.shape, lambda i: (0,) * a.ndim, pipeline_mode=pl.Buffered(1)
    )
    return pl.pallas_call(
        functools.partial(pixel_kernel, xt),
        out_shape=jax.ShapeDtypeStruct((height, 8 * wide), BF),
        grid=(pixels // xt,),
        in_specs=[whole(y), whole(yp), whole(table)],
        out_specs=pl.BlockSpec((height, 8 * wide), lambda i: (0, 0)),
        scratch_shapes=[
            pltpu.VMEM((2, 9, height, xt), BF),
            pltpu.VMEM((2, 4, height, pixels), BF),
        ],
        compiler_params=pltpu.CompilerParams(vmem_limit_bytes=VMEM_LIMIT),
    )(y, yp, table)


def body(nrows, nreal, nfield, sims, data, mask_flags, bins, cl_signal, cl_noise, norm, matching):
    height, npix = sims.shape[2:]
    kf, cols = bins.shape
    half, kh, jc = npix // 2, kf // 2, cols // 2
    top = height // 2
    row = lax.axis_index("rows")
    forward_scale = npix ** (-0.5)
    inverse_gain = kf ** (-0.5) / forward_scale

    freq = np.arange(kf) - kf // 2
    lanes_k, lanes_c = [], np.tile(np.repeat(np.arange(2), jc), nrows)
    for p in range(2):
        per_q = freq[p::2].reshape(nrows, 1, jc)
        lanes_k.append(np.broadcast_to(per_q, (nrows, 2, jc)).reshape(-1))
    ky_order = np.concatenate([freq[0::2], freq[1::2]])

    fx = []
    for p in range(2):
        c, s = outer_cis(0, half, lanes_k[p], npix)
        fx.append((jnp.where(lanes_c[None, :] == 0, c, -s) * forward_scale).astype(BF))
    fx = jnp.stack(fx)
    c, s = outer_cis(0, npix, ky_order, npix)
    cs = (jnp.concatenate([c, s], axis=1) * forward_scale).astype(BF)
    c, s = outer_cis(row * top, top, ky_order, npix)
    c = (c * forward_scale).astype(BF)
    s = (s * forward_scale).astype(BF)
    gain = jnp.asarray(inverse_gain * inverse_gain, BF)
    t8 = jnp.stack([jnp.concatenate([c[:, :kh], s[:, :kh]], axis=1),
                    jnp.concatenate([c[:, kh:], s[:, kh:]], axis=1)]) * gain
    c, s = outer_cis(row * top, top, freq, npix)
    local = (jnp.concatenate([c, s], axis=1) * forward_scale).astype(BF)
    sign = jnp.asarray(np.tile(1 - 2 * (freq % 2), 2)[None, :], BF)
    local = jnp.concatenate([local, local * sign], axis=0)
    fx, cs, t8, local = lax.optimization_barrier((fx, cs, t8, local))

    pick = np.zeros((cols, 2, 2, jc), np.float32)
    for p in range(2):
        for j in range(jc):
            pick[2 * j + p, p, :, j] = 1.0
    swap = np.zeros((kf, kf), np.float32)
    swap[np.arange(kf), ky_order + kf // 2] = 1.0
    moved = jnp.dot(jnp.asarray(swap, BF), bins.astype(BF), preferred_element_type=F32).astype(BF)
    moved = jnp.dot(
        moved, jnp.asarray(pick.reshape(cols, 4 * jc), BF), preferred_element_type=F32
    ).astype(BF)
    moved = moved.reshape(kf, 2, cols).transpose(1, 0, 2)
    cells = lax.all_gather(moved, "rows", axis=2, tiled=True)
    weight_vals = 1.0 / (cl_signal[0] + cl_noise[0])
    grad_vals = cl_signal[0] * weight_vals
    w, g = lookup(cells.reshape(2 * kf, kf), [weight_vals, grad_vals])
    w = w.reshape(2, kf, kf)
    g = g.reshape(2, kf, kf)
    step_size = 2.0 * math.pi / npix
    lx = jnp.asarray(np.stack(lanes_k)[:, None, :] * step_size, F32)
    ly = jnp.asarray(ky_order[None, :, None] * step_size, F32)
    gx, gy = lx * g, ly * g
    flat_bins = bins.reshape(-1, 128)
    ncell = lookup(flat_bins, [norm])[0].reshape(kf, cols)

    mask = jnp.repeat(jnp.repeat(mask_flags, TILE, axis=0), TILE, axis=1) > 0
    stacked = jnp.concatenate([sims[0], data], axis=0)
    masked = jnp.where(mask[None], stacked, jnp.zeros_like(stacked))
    lo, hi = masked[:, :, :half], masked[:, :, half:]
    flat = lambda a: a.reshape(2 * height, half)
    parts = [
        jnp.dot(flat(lo + hi), fx[0], preferred_element_type=F32).astype(BF),
        jnp.dot(flat(lo - hi), fx[1], preferred_element_type=F32).astype(BF),
    ]
    a = jnp.stack([v.reshape(2, height, nrows, cols) for v in parts])
    a = a.transpose(3, 2, 1, 0, 4).reshape(nrows * height, 4 * cols)
    a = lax.all_to_all(a, "rows", split_axis=0, concat_axis=0, tiled=True)
    pq = lax.dot_general(cs, a, (((0,), (0,)), ((), ())), preferred_element_type=F32)
    pq = pq.reshape(2, kf, 2, 2, 2, jc)
    x = jnp.stack(
        [pq[0, ..., 0, :] + pq[1, ..., 1, :], pq[0, ..., 1, :] - pq[1, ..., 0, :]], axis=3
    )
    x = x.astype(BF).transpose(1, 2, 0, 3, 4).reshape(2, 2, kf, cols)

    real = lax.axis_index("real")
    ids = jnp.arange(nreal, dtype=jnp.int32)
    partner = jnp.sum(jnp.where(ids == real, matching, 0))
    px = x[0]
    for shift in range(1, nreal):
        came = lax.ppermute(
            x[0], "real", [((d + shift) % nreal, d) for d in range(nreal)]
        )
        px = jnp.where(lax.rem(real + shift, nreal) == partner, came, px)

    both = lax.all_gather(x, "rows", axis=3, tiled=True)
    y = ky_inverse(both, w, gx, gy, t8, cols)
    other = lax.all_gather(px[None], "rows", axis=3, tiled=True)
    yp = ky_inverse(other, w, gx, gy, t8, cols)
    field_a = pixel_products(y, yp, fx)

    sums = lax.dot_general(local, field_a, (((0,), (0,)), ((), ())), preferred_element_type=F32)
    sums = sums.reshape(2, kf, 2, 2, 2, nrows, 2, jc)
    s_re = sums[0, ..., 0, :] + sums[1, ..., 1, :]
    s_im = sums[0, ..., 1, :] - sums[1, ..., 0, :]
    lxo = jnp.asarray(
        np.stack([freq[p::2] for p in range(2)]).reshape(1, 1, 2, nrows, jc) * step_size, F32
    )
    lyo = jnp.asarray(freq.reshape(kf, 1, 1, 1, 1) * step_size, F32)
    terms = jnp.stack(
        [
            -(lxo * s_im[:, 0] + lyo * s_im[:, 1]),
            lxo * s_re[:, 0] + lyo * s_re[:, 1],
        ],
        axis=2,
    ).astype(BF)
    terms = terms.transpose(4, 1, 2, 0, 3, 5).reshape(nrows * 4 * kf, cols)
    order = np.zeros((2, jc, cols), np.float32)
    for p in range(2):
        order[p, np.arange(jc), 2 * np.arange(jc) + p] = 1.0
    terms = jnp.dot(
        terms, jnp.asarray(order.reshape(cols, cols), BF), preferred_element_type=F32
    ).astype(BF)
    got = lax.all_to_all(terms, "rows", split_axis=0, concat_axis=0, tiled=True)
    got = jnp.sum(got.reshape(nrows, 2, 2, kf, cols).astype(F32), axis=0)
    mine = (got * ncell).astype(BF)
    total = mine.astype(F32)
    for shift in range(1, nfield):
        theirs = lax.ppermute(
            mine, "field", [(d, (d + shift) % nfield) for d in range(nfield)]
        )
        total = total + theirs.astype(F32)
    return total[None]


def solution(mesh):
    in_specs = (
        P("real", "field", "rows", None),
        P("field", "rows", None),
        P("rows", None),
        P(None, "rows"),
        P("field", None),
        P("field", None),
        P(),
        P(),
    )
    out_specs = P("real", None, None, None, "rows")
    f = functools.partial(body, mesh.shape["rows"], mesh.shape["real"], mesh.shape["field"])
    return jax.shard_map(f, mesh=mesh, in_specs=in_specs, out_specs=out_specs, check_vma=False)
```

```python
import functools
import math

import jax
import jax.numpy as jnp
import numpy as np
from jax import lax
from jax.experimental import pallas as pl
from jax.experimental.pallas import tpu as pltpu
from jax.sharding import PartitionSpec as P

TILE = 128
BF = jnp.bfloat16
F32 = jnp.float32
VMEM_LIMIT = 60 * 1024 * 1024


def cis(pixels, freqs, npix):
    phase = jnp.mod(pixels[:, None] * freqs[None, :], npix)
    angle = phase.astype(F32) * (2.0 * math.pi / npix)
    return jnp.cos(angle), jnp.sin(angle)


def outer_cis(start, count, freqs, npix, stride=1):
    low = 32
    freqs = jnp.asarray(freqs, jnp.int32)
    steps = low * stride * jnp.arange(count // low, dtype=jnp.int32)
    c1, s1 = cis(start + steps, freqs, npix)
    c0, s0 = cis(stride * jnp.arange(low, dtype=jnp.int32), freqs, npix)
    c1, s1, c0, s0 = lax.optimization_barrier((c1, s1, c0, s0))
    c1, s1, c0, s0 = c1[:, None], s1[:, None], c0[None], s0[None]
    width = freqs.shape[0]
    return (
        (c1 * c0 - s1 * s0).reshape(count, width),
        (s1 * c0 + c1 * s0).reshape(count, width),
    )


def lookup_kernel(idx_ref, tab_ref, *outs):
    idx = idx_ref[...].astype(jnp.int32)
    for t, out in enumerate(outs):
        table = jnp.broadcast_to(tab_ref[t : t + 1, :], idx.shape)
        out[...] = jnp.take_along_axis(table, idx, axis=1, mode="promise_in_bounds")


def lookup(idx, values):
    rows, width = idx.shape
    nbins = values[0].shape[0]
    tab = jnp.stack([jnp.pad(v, (0, 128 - nbins)) for v in values])
    tab = jnp.pad(tab, ((0, 8 - len(values)), (0, 0)))
    return pl.pallas_call(
        lookup_kernel,
        out_shape=[jax.ShapeDtypeStruct(idx.shape, F32) for _ in values],
        grid=(width // 128,),
        in_specs=[
            pl.BlockSpec((rows, 128), lambda i: (0, i)),
            pl.BlockSpec((8, 128), lambda i: (0, 0)),
        ],
        out_specs=[pl.BlockSpec((rows, 128), lambda i: (0, i)) for _ in values],
    )(idx, tab)


def forward_kernel(m_ref, mask_ref, f_ref, a_ref, even, odd):
    half = even.shape[1]
    cols = a_ref.shape[2] // 2
    for t in range(mask_ref.shape[0]):
        rows = pl.ds(t * TILE, TILE)
        lo = m_ref[rows, :half].astype(F32) * mask_ref[t : t + 1, :half]
        hi = m_ref[rows, half:].astype(F32) * mask_ref[t : t + 1, half:]
        even[rows, :] = (lo + hi).astype(BF)
        odd[rows, :] = (lo - hi).astype(BF)
    for p, side in enumerate((even, odd)):
        out = jnp.dot(side[...], f_ref[p], preferred_element_type=F32).astype(BF)
        for q in range(a_ref.shape[0]):
            a_ref[q, :, p * cols : (p + 1) * cols] = out[:, q * cols : (q + 1) * cols]


def forward(m, mask, table, nrows, cols):
    height, npix = m.shape
    return pl.pallas_call(
        forward_kernel,
        out_shape=jax.ShapeDtypeStruct((nrows, height, 2 * cols), BF),
        scratch_shapes=[pltpu.VMEM((height, npix // 2), BF)] * 2,
        compiler_params=pltpu.CompilerParams(vmem_limit_bytes=VMEM_LIMIT),
    )(m, mask, table)


def sum_kernel(cols, step_size, a_ref, t_ref, lx_ref, perm_ref, out_ref):
    kf = t_ref.shape[0] // 2
    shape = (kf, 128)
    ky = lax.broadcasted_iota(jnp.int32, shape, 0) - kf // 2
    ly = ky.astype(F32) * step_size
    first = (lax.broadcasted_iota(jnp.int32, shape, 1) & (cols - 1)) < cols // 2
    sides = []
    for p in range(2):
        lx = lx_ref[p]
        rhs = jnp.concatenate([a_ref[2 * i + p] for i in range(4)], axis=1)
        pq = jnp.dot(t_ref[...], rhs, preferred_element_type=F32)
        pairs = []
        for pair in range(2):
            x = pq[:, pair * 128 : (pair + 1) * 128]
            y = pq[:, (2 + pair) * 128 : (3 + pair) * 128]
            even = lx * x[:kf] + ly * y[:kf]
            turned = jnp.where(
                first,
                -pltpu.roll(even, 128 - cols // 2, axis=1),
                pltpu.roll(even, cols // 2, axis=1),
            )
            pairs.append((lx * x[kf:] + ly * y[kf:] + turned).astype(BF))
        sides.append(pairs)
    for pair in range(2):
        both = jnp.concatenate([sides[0][pair], sides[1][pair]], axis=1)
        moved = jnp.dot(both, perm_ref[...], preferred_element_type=F32).astype(BF)
        out_ref[0, pair, 0] = moved[:, :128]
        out_ref[0, pair, 1] = moved[:, 128:]


def row_sums(a, table, lx, perm, cols, step_size):
    _, height, wide = a.shape
    kf = table.shape[0] // 2
    blocks = wide // 128
    return pl.pallas_call(
        functools.partial(sum_kernel, cols, step_size),
        out_shape=jax.ShapeDtypeStruct((blocks, 2, 2, kf, 128), BF),
        grid=(blocks,),
        in_specs=[
            pl.BlockSpec((8, height, 128), lambda i: (0, 0, i)),
            pl.BlockSpec(table.shape, lambda i: (0, 0)),
            pl.BlockSpec((2, 1, 128), lambda i: (0, 0, i)),
            pl.BlockSpec(perm.shape, lambda i: (0, 0)),
        ],
        out_specs=pl.BlockSpec((1, 2, 2, kf, 128), lambda i: (i, 0, 0, 0, 0)),
        compiler_params=pltpu.CompilerParams(vmem_limit_bytes=VMEM_LIMIT),
    )(a, table, lx, perm)


def ky_kernel(cols, x_ref, w_ref, gx_ref, gy_ref, t_ref, y_ref):
    half = x_ref.shape[2] // 2
    top = y_ref.shape[2] // 2
    x = x_ref[0, 0].astype(F32)
    wide = x.shape[1]
    lane = lax.broadcasted_iota(jnp.int32, x.shape, 1)
    first = (lane & (cols - 1)) < cols // 2
    ix = jnp.where(
        first, -pltpu.roll(x, wide - cols // 2, axis=1), pltpu.roll(x, cols // 2, axis=1)
    )
    w, gx, gy = w_ref[0], gx_ref[0], gy_ref[0]
    pairs = ((w * x, w * ix), (gx * ix, -(gx * x)), (gy * ix, -(gy * x)))
    for leg, (z, iz) in enumerate(pairs):
        z = z.astype(BF)
        iz = iz.astype(BF)
        even = jnp.dot(
            t_ref[0], jnp.concatenate([z[:half], iz[:half]], axis=0), preferred_element_type=F32
        )
        odd = jnp.dot(
            t_ref[1], jnp.concatenate([z[half:], iz[half:]], axis=0), preferred_element_type=F32
        )
        y_ref[0, leg, :top, :] = (even + odd).astype(BF)
        y_ref[0, leg, top:, :] = (even - odd).astype(BF)


def ky_inverse(x, w, gx, gy, table, cols):
    maps, _, kf, wide = x.shape
    top = table.shape[1]
    lanes = 256
    blocks = wide // lanes
    cell = pl.BlockSpec((1, kf, lanes), lambda p, i, m: (p, 0, i))
    return pl.pallas_call(
        functools.partial(ky_kernel, cols),
        out_shape=jax.ShapeDtypeStruct((maps, 3, 2 * top, 2 * wide), BF),
        grid=(2, blocks, maps),
        in_specs=[
            pl.BlockSpec((1, 1, kf, lanes), lambda p, i, m: (m, p, 0, i)),
            cell,
            cell,
            cell,
            pl.BlockSpec(table.shape, lambda p, i, m: (0, 0, 0)),
        ],
        out_specs=pl.BlockSpec(
            (1, 3, 2 * top, lanes), lambda p, i, m: (m, 0, 0, p * blocks + i)
        ),
        compiler_params=pltpu.CompilerParams(vmem_limit_bytes=VMEM_LIMIT),
    )(x, w, gx, gy, table)


def pixel_kernel(xt, ys_ref, yd_ref, yp_ref, f_ref, a_ref, legs, prods):
    step = pl.program_id(0)
    height = ys_ref.shape[2]
    wide = f_ref.shape[2]
    here = pl.ds(pl.multiple_of(step * xt, xt), xt)
    dims = (((1,), (1,)), ((), ()))

    def make(source, leg, slot):
        even = lax.dot_general(
            source[0, leg, :, :wide], f_ref[0, here, :], dims, preferred_element_type=F32
        )
        odd = lax.dot_general(
            source[0, leg, :, wide:], f_ref[1, here, :], dims, preferred_element_type=F32
        )
        legs[0, slot] = (even + odd).astype(BF)
        legs[1, slot] = (even - odd).astype(BF)

    @pl.loop(0, 3)
    def _(leg):
        make(ys_ref, leg, leg)
        make(yd_ref, leg, leg + 3)
        make(yp_ref, leg, leg + 6)

    chunk = 64

    @pl.loop(0, height // chunk)
    def _(c):
        rows = pl.ds(pl.multiple_of(c * chunk, chunk), chunk)
        sides = []
        for side in range(2):
            own = [legs[side, i, rows, :].astype(F32) for i in range(3)]
            dat = [legs[side, i + 3, rows, :].astype(F32) for i in range(3)]
            par = [legs[side, i + 6, rows, :].astype(F32) for i in range(3)]
            sides.append(
                (
                    dat[1] * own[0] + own[1] * dat[0],
                    own[1] * par[0] + par[1] * own[0],
                    dat[2] * own[0] + own[2] * dat[0],
                    own[2] * par[0] + par[2] * own[0],
                )
            )
        for i in range(4):
            prods[0, i, rows, here] = (sides[0][i] + sides[1][i]).astype(BF)
            prods[1, i, rows, here] = (sides[0][i] - sides[1][i]).astype(BF)

    @pl.when(step == pl.num_programs(0) - 1)
    def _():
        @pl.loop(0, 4)
        def _(i):
            for p in range(2):
                a_ref[2 * i + p] = jnp.dot(
                    prods[p, i], f_ref[p], preferred_element_type=F32
                ).astype(BF)


def pixel_products(ys, yd, yp, table):
    height = ys.shape[2]
    pixels, wide = table.shape[1:]
    xt = 256
    whole = lambda a: pl.BlockSpec(
        a.shape, lambda i: (0,) * a.ndim, pipeline_mode=pl.Buffered(1)
    )
    return pl.pallas_call(
        functools.partial(pixel_kernel, xt),
        out_shape=jax.ShapeDtypeStruct((8, height, wide), BF),
        grid=(pixels // xt,),
        in_specs=[whole(ys), whole(yd), whole(yp), whole(table)],
        out_specs=pl.BlockSpec((8, height, wide), lambda i: (0, 0, 0)),
        scratch_shapes=[
            pltpu.VMEM((2, 9, height, xt), BF),
            pltpu.VMEM((2, 4, height, pixels), BF),
        ],
        compiler_params=pltpu.CompilerParams(vmem_limit_bytes=VMEM_LIMIT),
    )(ys, yd, yp, table)


def body(nrows, nreal, nfield, sims, data, mask_flags, bins, cl_signal, cl_noise, norm, matching):
    height, npix = sims.shape[2:]
    kf, cols = bins.shape
    half, kh, jc = npix // 2, kf // 2, cols // 2
    top = height // 2
    row = lax.axis_index("rows")
    forward_scale = npix ** (-0.5)
    inverse_gain = kf ** (-0.5) / forward_scale

    freq = np.arange(kf) - kf // 2
    lanes_k, lanes_c = [], np.tile(np.repeat(np.arange(2), jc), nrows)
    for p in range(2):
        per_q = freq[p::2].reshape(nrows, 1, jc)
        lanes_k.append(np.broadcast_to(per_q, (nrows, 2, jc)).reshape(-1))
    ky_order = np.concatenate([freq[0::2], freq[1::2]])

    fx = []
    for p in range(2):
        c, s = outer_cis(0, half, lanes_k[p], npix)
        fx.append((jnp.where(lanes_c[None, :] == 0, c, -s) * forward_scale).astype(BF))
    fx = jnp.stack(fx)
    every = np.arange(npix)
    halves = [outer_cis(p - kf // 2, kh, every, npix, stride=2) for p in range(2)]
    cs = (
        jnp.concatenate([halves[0][0], halves[1][0], halves[0][1], halves[1][1]], axis=0)
        * forward_scale
    ).astype(BF)
    c, s = outer_cis(row * top, top, ky_order, npix)
    c = (c * forward_scale).astype(BF)
    s = (s * forward_scale).astype(BF)
    gain = jnp.asarray(inverse_gain * inverse_gain, BF)
    t8 = jnp.stack([jnp.concatenate([c[:, :kh], s[:, :kh]], axis=1),
                    jnp.concatenate([c[:, kh:], s[:, kh:]], axis=1)]) * gain
    near = row * top + jnp.arange(top, dtype=jnp.int32)
    c, s = outer_cis(-(kf // 2), kf, jnp.concatenate([near, near + half]), npix)
    local = (jnp.concatenate([c, s], axis=0) * forward_scale).astype(BF)
    fx, cs, t8, local = lax.optimization_barrier((fx, cs, t8, local))

    pick = np.zeros((cols, 2, 2, jc), np.float32)
    for p in range(2):
        for j in range(jc):
            pick[2 * j + p, p, :, j] = 1.0
    swap = np.zeros((kf, kf), np.float32)
    swap[np.arange(kf), ky_order + kf // 2] = 1.0
    moved = jnp.dot(jnp.asarray(swap, BF), bins.astype(BF), preferred_element_type=F32).astype(BF)
    moved = jnp.dot(
        moved, jnp.asarray(pick.reshape(cols, 4 * jc), BF), preferred_element_type=F32
    ).astype(BF)
    moved = moved.reshape(kf, 2, cols).transpose(1, 0, 2)
    cells = lax.all_gather(moved, "rows", axis=2, tiled=True)
    weight_vals = 1.0 / (cl_signal[0] + cl_noise[0])
    grad_vals = cl_signal[0] * weight_vals
    w, g = lookup(cells.reshape(2 * kf, kf), [weight_vals, grad_vals])
    w = w.reshape(2, kf, kf)
    g = g.reshape(2, kf, kf)
    step_size = 2.0 * math.pi / npix
    lx = jnp.asarray(np.stack(lanes_k)[:, None, :] * step_size, F32)
    ly = jnp.asarray(ky_order[None, :, None] * step_size, F32)
    gx, gy = lx * g, ly * g
    flat_bins = bins.reshape(-1, 128)
    ncell = lookup(flat_bins, [norm])[0].reshape(kf, cols)

    mask = jnp.repeat(mask_flags.astype(F32), TILE, axis=1)

    def cells_of(m):
        a = forward(m, mask, fx, nrows, cols).reshape(nrows * height, 2 * cols)
        a = lax.all_to_all(a, "rows", split_axis=0, concat_axis=0, tiled=True)
        pq = jnp.dot(cs, a, preferred_element_type=F32).reshape(2, kf, 2, 2, jc)
        x = jnp.stack(
            [pq[0, ..., 0, :] + pq[1, ..., 1, :], pq[0, ..., 1, :] - pq[1, ..., 0, :]], axis=2
        )
        return x.astype(BF).transpose(1, 0, 2, 3).reshape(2, kf, cols)

    def ky_part(cells):
        full = lax.all_gather(cells[None], "rows", axis=3, tiled=True)
        return ky_inverse(full, w, gx, gy, t8, cols)

    x = cells_of(sims[0, 0])
    xd = cells_of(data[0])

    real = lax.axis_index("real")
    ids = jnp.arange(nreal, dtype=jnp.int32)
    partner = jnp.sum(jnp.where(ids == real, matching, 0))
    px = x
    for shift in range(1, nreal):
        came = lax.ppermute(
            x, "real", [((d + shift) % nreal, d) for d in range(nreal)]
        )
        px = jnp.where(lax.rem(real + shift, nreal) == partner, came, px)

    ys = ky_part(x)
    yd = ky_part(xd)
    yp = ky_part(px)
    field_a = pixel_products(ys, yd, yp, fx)

    perm = np.zeros((2, 128, 2, 128), np.float32)
    at = np.arange(128)
    for p in range(2):
        perm[p, at, at % cols // jc, at // cols * cols + 2 * (at % jc) + p] = 1.0
    perm = jnp.asarray(perm.reshape(256, 256), BF)
    terms = row_sums(field_a, local, lx, perm, cols, step_size)
    terms = terms.reshape(-1, 2, 2, kf, 128 // cols, cols).transpose(0, 4, 1, 2, 3, 5)
    terms = terms.reshape(nrows * 4 * kf, cols)
    got = lax.all_to_all(terms, "rows", split_axis=0, concat_axis=0, tiled=True)
    got = jnp.sum(got.reshape(nrows, 2, 2, kf, cols).astype(F32), axis=0)
    mine = (got * ncell).astype(BF)
    total = mine.astype(F32)
    for shift in range(1, nfield):
        theirs = lax.ppermute(
            mine, "field", [(d, (d + shift) % nfield) for d in range(nfield)]
        )
        total = total + theirs.astype(F32)
    return total[None]


def solution(mesh):
    in_specs = (
        P("real", "field", "rows", None),
        P("field", "rows", None),
        P("rows", None),
        P(None, "rows"),
        P("field", None),
        P("field", None),
        P(),
        P(),
    )
    out_specs = P("real", None, None, None, "rows")
    f = functools.partial(body, mesh.shape["rows"], mesh.shape["real"], mesh.shape["field"])
    return jax.shard_map(f, mesh=mesh, in_specs=in_specs, out_specs=out_specs, check_vma=False)
```

```python
import functools
import math

import jax
import jax.numpy as jnp
import numpy as np
from jax import lax
from jax.experimental import pallas as pl
from jax.experimental.pallas import tpu as pltpu
from jax.sharding import PartitionSpec as P

TILE = 128
BF = jnp.bfloat16
F32 = jnp.float32
VMEM_LIMIT = 60 * 1024 * 1024


def cis(pixels, freqs, npix):
    phase = np.mod(np.asarray(pixels)[..., :, None] * np.asarray(freqs)[..., None, :], npix)
    angle = phase * (2.0 * math.pi / npix)
    return np.cos(angle).astype(np.float32), np.sin(angle).astype(np.float32)


def product_table(high, low):
    c1, s1 = (jnp.asarray(v)[:, None] for v in high)
    c0, s0 = (jnp.asarray(v)[None] for v in low)
    shape = (c1.shape[0] * c0.shape[1], c0.shape[2])
    return (c1 * c0 - s1 * s0).reshape(shape), (s1 * c0 + c1 * s0).reshape(shape)


def outer_cis(start, count, freqs, npix, stride=1, low=32):
    high = start + low * stride * np.arange(count // low)
    return product_table(cis(high, freqs, npix), cis(stride * np.arange(low), freqs, npix))


def lookup_kernel(idx_ref, tab_ref, *outs):
    idx = idx_ref[...].astype(jnp.int32)
    for t, out in enumerate(outs):
        table = jnp.broadcast_to(tab_ref[t : t + 1, :], idx.shape)
        out[...] = jnp.take_along_axis(table, idx, axis=1, mode="promise_in_bounds")


def lookup(idx, values):
    rows, width = idx.shape
    nbins = values[0].shape[0]
    tab = jnp.stack([jnp.pad(v, (0, 128 - nbins)) for v in values])
    tab = jnp.pad(tab, ((0, 8 - len(values)), (0, 0)))
    return pl.pallas_call(
        lookup_kernel,
        out_shape=[jax.ShapeDtypeStruct(idx.shape, F32) for _ in values],
        grid=(width // 128,),
        in_specs=[
            pl.BlockSpec((rows, 128), lambda i: (0, i)),
            pl.BlockSpec((8, 128), lambda i: (0, 0)),
        ],
        out_specs=[pl.BlockSpec((rows, 128), lambda i: (0, i)) for _ in values],
        cost_estimate=pl.CostEstimate(
            flops=rows * width, bytes_accessed=16 * rows * width, transcendentals=0
        ),
    )(idx, tab)


def forward_kernel(m_ref, mask_ref, f_ref, a_ref, even, odd):
    half = even.shape[1]
    cols = a_ref.shape[2] // 2
    for t in range(mask_ref.shape[0]):
        rows = pl.ds(t * TILE, TILE)
        lo = m_ref[rows, :half].astype(F32) * mask_ref[t : t + 1, :half]
        hi = m_ref[rows, half:].astype(F32) * mask_ref[t : t + 1, half:]
        even[rows, :] = (lo + hi).astype(BF)
        odd[rows, :] = (lo - hi).astype(BF)
    for p, side in enumerate((even, odd)):
        out = jnp.dot(side[...], f_ref[p], preferred_element_type=F32).astype(BF)
        for q in range(a_ref.shape[0]):
            a_ref[q, :, p * cols : (p + 1) * cols] = out[:, q * cols : (q + 1) * cols]


def forward(m, mask, table, nrows, cols):
    height, npix = m.shape
    return pl.pallas_call(
        forward_kernel,
        out_shape=jax.ShapeDtypeStruct((nrows, height, 2 * cols), BF),
        scratch_shapes=[pltpu.VMEM((height, npix // 2), BF)] * 2,
        compiler_params=pltpu.CompilerParams(vmem_limit_bytes=VMEM_LIMIT),
        cost_estimate=pl.CostEstimate(
            flops=4 * height * npix * nrows * cols,
            bytes_accessed=4 * height * npix,
            transcendentals=0,
        ),
    )(m, mask, table)


def sum_kernel(cols, step_size, a_ref, t_ref, lx_ref, perm_ref, out_ref):
    kf = t_ref.shape[0] // 2
    shape = (kf, 128)
    ky = lax.broadcasted_iota(jnp.int32, shape, 0) - kf // 2
    ly = ky.astype(F32) * step_size
    first = (lax.broadcasted_iota(jnp.int32, shape, 1) & (cols - 1)) < cols // 2
    sides = []
    for p in range(2):
        lx = lx_ref[p]
        rhs = jnp.concatenate([a_ref[2 * i + p] for i in range(2)], axis=1)
        pq = jnp.dot(t_ref[...], rhs, preferred_element_type=F32)
        x, y = pq[:, :128], pq[:, 128:]
        even = lx * x[:kf] + ly * y[:kf]
        turned = jnp.where(
            first,
            -pltpu.roll(even, 128 - cols // 2, axis=1),
            pltpu.roll(even, cols // 2, axis=1),
        )
        sides.append((lx * x[kf:] + ly * y[kf:] + turned).astype(BF))
    both = jnp.concatenate(sides, axis=1)
    moved = jnp.dot(both, perm_ref[...], preferred_element_type=F32).astype(BF)
    out_ref[0, 0] = moved[:, :128]
    out_ref[0, 1] = moved[:, 128:]


def row_sums(a, table, lx, perm, cols, step_size):
    _, height, wide = a.shape
    kf = table.shape[0] // 2
    blocks = wide // 128
    return pl.pallas_call(
        functools.partial(sum_kernel, cols, step_size),
        out_shape=jax.ShapeDtypeStruct((blocks, 2, kf, 128), BF),
        grid=(blocks,),
        in_specs=[
            pl.BlockSpec((4, height, 128), lambda i: (0, 0, i)),
            pl.BlockSpec(table.shape, lambda i: (0, 0)),
            pl.BlockSpec((2, 1, 128), lambda i: (0, 0, i)),
            pl.BlockSpec(perm.shape, lambda i: (0, 0)),
        ],
        out_specs=pl.BlockSpec((1, 2, kf, 128), lambda i: (i, 0, 0, 0)),
        compiler_params=pltpu.CompilerParams(vmem_limit_bytes=VMEM_LIMIT),
        cost_estimate=pl.CostEstimate(
            flops=2 * height * 2 * kf * 4 * wide, bytes_accessed=12 * wide * kf, transcendentals=0
        ),
    )(a, table, lx, perm)


def ky_kernel(cols, x_ref, w_ref, gx_ref, gy_ref, t_ref, y_ref):
    half = x_ref.shape[2] // 2
    top = y_ref.shape[2] // 2
    x = x_ref[0, 0].astype(F32)
    wide = x.shape[1]
    lane = lax.broadcasted_iota(jnp.int32, x.shape, 1)
    first = (lane & (cols - 1)) < cols // 2
    ix = jnp.where(
        first, -pltpu.roll(x, wide - cols // 2, axis=1), pltpu.roll(x, cols // 2, axis=1)
    )
    w, gx, gy = w_ref[0], gx_ref[0], gy_ref[0]
    pairs = ((w * x, w * ix), (gx * ix, -(gx * x)), (gy * ix, -(gy * x)))
    for leg, (z, iz) in enumerate(pairs):
        z = z.astype(BF)
        iz = iz.astype(BF)
        even = jnp.dot(
            t_ref[0], jnp.concatenate([z[:half], iz[:half]], axis=0), preferred_element_type=F32
        )
        odd = jnp.dot(
            t_ref[1], jnp.concatenate([z[half:], iz[half:]], axis=0), preferred_element_type=F32
        )
        y_ref[0, leg, :top, :] = (even + odd).astype(BF)
        y_ref[0, leg, top:, :] = (even - odd).astype(BF)


def ky_inverse(x, w, gx, gy, table, cols):
    maps, _, kf, wide = x.shape
    top = table.shape[1]
    lanes = 256
    blocks = wide // lanes
    cell = pl.BlockSpec((1, kf, lanes), lambda p, i, m: (p, 0, i))
    return pl.pallas_call(
        functools.partial(ky_kernel, cols),
        out_shape=jax.ShapeDtypeStruct((maps, 3, 2 * top, 2 * wide), BF),
        grid=(2, blocks, maps),
        in_specs=[
            pl.BlockSpec((1, 1, kf, lanes), lambda p, i, m: (m, p, 0, i)),
            cell,
            cell,
            cell,
            pl.BlockSpec(table.shape, lambda p, i, m: (0, 0, 0)),
        ],
        out_specs=pl.BlockSpec(
            (1, 3, 2 * top, lanes), lambda p, i, m: (m, 0, 0, p * blocks + i)
        ),
        compiler_params=pltpu.CompilerParams(vmem_limit_bytes=VMEM_LIMIT),
        cost_estimate=pl.CostEstimate(
            flops=3 * 16 * maps * top * kf * wide,
            bytes_accessed=48 * kf * wide,
            transcendentals=0,
        ),
    )(x, w, gx, gy, table)


DIMS = (((1,), (1,)), ((), ()))


def make_legs(source, f_ref, here, dest):
    wide = f_ref.shape[2]

    @pl.loop(0, 3)
    def _(leg):
        even = lax.dot_general(
            source[0, leg, :, :wide], f_ref[0, here, :], DIMS, preferred_element_type=F32
        )
        odd = lax.dot_general(
            source[0, leg, :, wide:], f_ref[1, here, :], DIMS, preferred_element_type=F32
        )
        dest[0, leg] = (even + odd).astype(BF)
        dest[1, leg] = (even - odd).astype(BF)


def make_products(own_ref, other_ref, prods, here):
    height = own_ref.shape[2]
    chunk = 64

    @pl.loop(0, height // chunk)
    def _(c):
        rows = pl.ds(pl.multiple_of(c * chunk, chunk), chunk)
        sides = []
        for side in range(2):
            own = [own_ref[side, i, rows, :].astype(F32) for i in range(3)]
            other = [other_ref[side, i, rows, :].astype(F32) for i in range(3)]
            sides.append([other[d] * own[0] + own[d] * other[0] for d in (1, 2)])
        for i in range(2):
            prods[0, i, rows, here] = (sides[0][i] + sides[1][i]).astype(BF)
            prods[1, i, rows, here] = (sides[0][i] - sides[1][i]).astype(BF)


def transform_products(prods, f_ref, a_ref):
    @pl.when(pl.program_id(0) == pl.num_programs(0) - 1)
    def _():
        @pl.loop(0, 2)
        def _(i):
            for p in range(2):
                a_ref[2 * i + p] = jnp.dot(
                    prods[p, i], f_ref[p], preferred_element_type=F32
                ).astype(BF)


def first_kernel(xt, ys_ref, yd_ref, f_ref, a_ref, own_ref, other, prods):
    here = pl.ds(pl.multiple_of(pl.program_id(0) * xt, xt), xt)
    make_legs(ys_ref, f_ref, here, own_ref)
    make_legs(yd_ref, f_ref, here, other)
    make_products(own_ref, other, prods, here)
    transform_products(prods, f_ref, a_ref)


def second_kernel(xt, yp_ref, own_ref, f_ref, a_ref, other, prods):
    here = pl.ds(pl.multiple_of(pl.program_id(0) * xt, xt), xt)
    make_legs(yp_ref, f_ref, here, other)
    make_products(own_ref, other, prods, here)
    transform_products(prods, f_ref, a_ref)


def pixel_products(own, other, table, first):
    height = other.shape[2]
    pixels, wide = table.shape[1:]
    xt = 256
    whole = lambda a: pl.BlockSpec(
        a.shape, lambda i: (0,) * a.ndim, pipeline_mode=pl.Buffered(1)
    )
    legs_spec = pl.BlockSpec((2, 3, height, xt), lambda i: (0, 0, 0, i))
    a_shape = jax.ShapeDtypeStruct((4, height, wide), BF)
    a_spec = pl.BlockSpec((4, height, wide), lambda i: (0, 0, 0))
    maps = 2 if first else 1
    params = dict(
        grid=(pixels // xt,),
        scratch_shapes=[
            pltpu.VMEM((2, 3, height, xt), BF),
            pltpu.VMEM((2, 2, height, pixels), BF),
        ],
        compiler_params=pltpu.CompilerParams(vmem_limit_bytes=VMEM_LIMIT),
        cost_estimate=pl.CostEstimate(
            flops=2 * height * pixels * wide * (6 * maps + 4),
            bytes_accessed=2 * height * pixels * 12,
            transcendentals=0,
        ),
    )
    if first:
        legs_shape = jax.ShapeDtypeStruct((2, 3, height, pixels), BF)
        return pl.pallas_call(
            functools.partial(first_kernel, xt),
            out_shape=[a_shape, legs_shape],
            in_specs=[whole(own), whole(other), whole(table)],
            out_specs=[a_spec, legs_spec],
            **params,
        )(own, other, table)
    return pl.pallas_call(
        functools.partial(second_kernel, xt),
        out_shape=a_shape,
        in_specs=[whole(other), legs_spec, whole(table)],
        out_specs=a_spec,
        **params,
    )(other, own, table)


def body(nrows, nreal, nfield, sims, data, mask_flags, bins, cl_signal, cl_noise, norm, matching):
    height, npix = sims.shape[2:]
    kf, cols = bins.shape
    half, kh, jc = npix // 2, kf // 2, cols // 2
    top = height // 2
    row = lax.axis_index("rows")
    forward_scale = npix ** (-0.5)
    inverse_gain = kf ** (-0.5) / forward_scale

    freq = np.arange(kf) - kf // 2
    lanes_k, lanes_c = [], np.tile(np.repeat(np.arange(2), jc), nrows)
    for p in range(2):
        per_q = freq[p::2].reshape(nrows, 1, jc)
        lanes_k.append(np.broadcast_to(per_q, (nrows, 2, jc)).reshape(-1))
    ky_order = np.concatenate([freq[0::2], freq[1::2]])

    fx = []
    for p in range(2):
        c, s = outer_cis(0, half, lanes_k[p], npix)
        fx.append((jnp.where(lanes_c[None, :] == 0, c, -s) * forward_scale).astype(BF))
    fx = jnp.stack(fx)
    every = np.arange(npix)
    halves = [outer_cis(p - kf // 2, kh, every, npix, stride=2) for p in range(2)]
    cs = (
        jnp.concatenate([halves[0][0], halves[1][0], halves[0][1], halves[1][1]], axis=0)
        * forward_scale
    ).astype(BF)
    low = 32
    starts = np.arange(nrows)[:, None] * top + low * np.arange(top // low)
    high = [
        lax.dynamic_index_in_dim(jnp.asarray(v), row, keepdims=False)
        for v in cis(starts, ky_order, npix)
    ]
    c, s = product_table(high, cis(np.arange(low), ky_order, npix))
    c = (c * forward_scale).astype(BF)
    s = (s * forward_scale).astype(BF)
    gain = jnp.asarray(inverse_gain * inverse_gain, BF)
    t8 = jnp.stack([jnp.concatenate([c[:, :kh], s[:, :kh]], axis=1),
                    jnp.concatenate([c[:, kh:], s[:, kh:]], axis=1)]) * gain
    near = np.arange(nrows)[:, None] * top + np.arange(top)
    near = np.concatenate([near, near + half], axis=1)
    pieces = []
    for ks in (low * np.arange(kf // low) - kf // 2, np.arange(low)):
        ks = np.broadcast_to(ks, (nrows, ks.shape[0]))
        pieces.append(
            [
                lax.dynamic_index_in_dim(jnp.asarray(v), row, keepdims=False)
                for v in cis(ks, near, npix)
            ]
        )
    c, s = product_table(*pieces)
    local = (jnp.concatenate([c, s], axis=0) * forward_scale).astype(BF)
    fx = lax.optimization_barrier(fx)
    cs = lax.optimization_barrier(cs)
    t8 = lax.optimization_barrier(t8)
    local = lax.optimization_barrier(local)

    pick = np.zeros((cols, 2, 2, jc), np.float32)
    for p in range(2):
        for j in range(jc):
            pick[2 * j + p, p, :, j] = 1.0
    swap = np.zeros((kf, kf), np.float32)
    swap[np.arange(kf), ky_order + kf // 2] = 1.0
    moved = jnp.dot(jnp.asarray(swap, BF), bins.astype(BF), preferred_element_type=F32).astype(BF)
    moved = jnp.dot(
        moved, jnp.asarray(pick.reshape(cols, 4 * jc), BF), preferred_element_type=F32
    ).astype(BF)
    moved = moved.reshape(kf, 2, cols).transpose(1, 0, 2)
    cells = lax.all_gather(moved, "rows", axis=2, tiled=True)
    weight_vals = 1.0 / (cl_signal[0] + cl_noise[0])
    grad_vals = cl_signal[0] * weight_vals
    w, g = lookup(cells.reshape(2 * kf, kf), [weight_vals, grad_vals])
    w = w.reshape(2, kf, kf)
    g = g.reshape(2, kf, kf)
    step_size = 2.0 * math.pi / npix
    lx = jnp.asarray(np.stack(lanes_k)[:, None, :] * step_size, F32)
    ly = jnp.asarray(ky_order[None, :, None] * step_size, F32)
    gx, gy = lx * g, ly * g
    flat_bins = bins.reshape(-1, 128)
    ncell = lookup(flat_bins, [norm])[0].reshape(kf, cols)

    mask = jnp.repeat(mask_flags.astype(F32), TILE, axis=1)

    def exchange(a):
        a = a.reshape(nrows * height, 2 * cols)
        return lax.all_to_all(a, "rows", split_axis=0, concat_axis=0, tiled=True)

    def cells_of(a):
        pq = jnp.dot(cs, a, preferred_element_type=F32).reshape(2, kf, 2, 2, jc)
        x = jnp.stack(
            [pq[0, ..., 0, :] + pq[1, ..., 1, :], pq[0, ..., 1, :] - pq[1, ..., 0, :]], axis=2
        )
        return x.astype(BF).transpose(1, 0, 2, 3).reshape(2, kf, cols)

    def ky_part(cells):
        full = lax.all_gather(cells[None], "rows", axis=3, tiled=True)
        return ky_inverse(full, w, gx, gy, t8, cols)

    own_a = forward(sims[0, 0], mask, fx, nrows, cols)
    own_a, second = lax.optimization_barrier((own_a, data[0]))
    data_a = forward(second, mask, fx, nrows, cols)
    own_a, w, gx, gy, cs = lax.optimization_barrier((exchange(own_a), w, gx, gy, cs))
    own_a, data_a = lax.optimization_barrier((own_a, data_a))
    x = cells_of(own_a)
    xd = cells_of(exchange(data_a))

    real = lax.axis_index("real")
    ids = jnp.arange(nreal, dtype=jnp.int32)
    partner = jnp.sum(jnp.where(ids == real, matching, 0))
    px = x
    for shift in range(1, nreal):
        came = lax.ppermute(
            x, "real", [((d + shift) % nreal, d) for d in range(nreal)]
        )
        px = jnp.where(lax.rem(real + shift, nreal) == partner, came, px)

    ys = ky_part(x)
    yd = ky_part(xd)
    yp = ky_part(px)
    first_a, own_legs = pixel_products(ys, yd, fx, True)

    perm = np.zeros((2, 128, 2, 128), np.float32)
    at = np.arange(128)
    for p in range(2):
        perm[p, at, at % cols // jc, at // cols * cols + 2 * (at % jc) + p] = 1.0
    perm = jnp.asarray(perm.reshape(256, 256), BF)

    def partial_sums(field_a):
        terms = row_sums(field_a, local, lx, perm, cols, step_size)
        terms = terms.reshape(-1, 2, kf, 128 // cols, cols).transpose(0, 3, 1, 2, 4)
        return terms.reshape(nrows * 2 * kf, cols)

    def over_rows(terms):
        got = lax.all_to_all(terms, "rows", split_axis=0, concat_axis=0, tiled=True)
        got = jnp.sum(got.reshape(nrows, 2, kf, cols).astype(F32), axis=0)
        return (got * ncell).astype(BF)

    def over_field(mine):
        total = mine.astype(F32)
        for shift in range(1, nfield):
            theirs = lax.ppermute(
                mine, "field", [(d, (d + shift) % nfield) for d in range(nfield)]
            )
            total = total + theirs.astype(F32)
        return total

    terms = partial_sums(first_a)
    terms, own_legs, yp = lax.optimization_barrier((terms, own_legs, yp))
    mine = over_rows(terms)
    second_terms = partial_sums(pixel_products(own_legs, yp, fx, False))
    mine, second_terms = lax.optimization_barrier((mine, second_terms))
    second_mine = over_rows(second_terms)
    return jnp.stack([over_field(mine), over_field(second_mine)])[None]


def solution(mesh):
    in_specs = (
        P("real", "field", "rows", None),
        P("field", "rows", None),
        P("rows", None),
        P(None, "rows"),
        P("field", None),
        P("field", None),
        P(),
        P(),
    )
    out_specs = P("real", None, None, None, "rows")
    f = functools.partial(body, mesh.shape["rows"], mesh.shape["real"], mesh.shape["field"])
    return jax.shard_map(f, mesh=mesh, in_specs=in_specs, out_specs=out_specs, check_vma=False)
```
